256 devices in a mesh: tm: 64 (over y_lo, x, z), panel: 4 (over y_hi, core).
Axes of the slice: x: 4, y: 4 (y_hi: 2, y_lo: 2; y = y_hi * 2 + y_lo), z: 8, core: 2. Of those that a mesh axis runs over, the one named last changes fastest.
Arguments:
- spins: int32 [64, 1152], P('tm'), may hold values from -1 to 1, as said below
- neighbours: int32 [1152, 4], replicated, may hold values from 0 to 1151, as said below
- start: float32 [73728, 1152], P(('tm', 'panel')), may hold values from -6 to 6
Outputs:
- panels: float32 [73728, 1152], P(('tm', 'panel'))
- growth: float32 [73728], P(('tm', 'panel'))
The draws below stay inside these ranges and needn't reach their ends.
Inputs may be any that keep to these rules, and one draw needn't show every extreme that they name: `spins`: each entry is -1 or +1. The nearest neighbours of a periodic (24) x 48 square lattice whose sites carry a random labelling; the table is symmetric.
All inputs are finite; a program needn't handle non-finite values.
Results may differ from the reference program's by a relative error of at most 0.0092.
Values may be sent and summed in bfloat16 or wider, within the bound.
No kernel may reach another device: no remote copies, remote signals or barrier semaphores. Data moves between devices by JAX's collectives and lax.ppermute only.
A program may use at most 64 MiB of HBM per device.

```python
import jax
import jax.numpy as jnp
from jax import lax

N = 1152
SLICES = 64
STEPS = 4


def draw_spins(key, part):
    values = jax.random.randint(key, (SLICES, N), 0, 2)
    return (2 * values - 1).astype(jnp.int32)


def draw_neighbours(key, part):
    order = jax.random.permutation(key, N).astype(jnp.int32)
    place = jnp.arange(N, dtype=jnp.int32)
    height = N // 48
    line = place // 48
    column = place % 48
    beside = jnp.stack([(line + 1) % height * 48 + column, (line + height - 1) % height * 48 + column, line * 48 + (column + 1) % 48, line * 48 + (column + 47) % 48], axis=1)
    table = jnp.zeros((N, 4), jnp.int32).at[order].set(order[beside])
    return table.astype(jnp.int32)


def levels(stream_key, shape, pieces, smallest, top_value):
    def one(dim, shards_of):
        heights = jax.random.uniform(jax.random.fold_in(jax.random.fold_in(stream_key, 6), dim), (shards_of,), jnp.float32, smallest / len(pieces), top_value / len(pieces))
        return jnp.repeat(jnp.exp(heights), shape[dim] // shards_of).reshape((-1,) + (1,) * (len(shape) - dim - 1))

    loudness = one(*pieces[0])
    for cut in pieces[1:]:
        loudness = loudness * one(*cut)
    return loudness


def bell_draw(rng, extent, scale, most, cuts=(), held_as=jnp.bfloat16):
    values = jax.random.normal(rng, extent, jnp.float32) * scale
    if len(cuts) > 0:
        values = levels(rng, extent, cuts, -0.22, 0.18) * values
    return jnp.clip(values, min=-most, max=most).astype(held_as)


def setup_inputs(seed: int = 0) -> dict:
    key_of = jax.random.split(jax.random.key(seed), 4)
    return {
        "spins": draw_spins(jax.random.fold_in(key_of[3], 71), 0),
        "neighbours": draw_neighbours(jax.random.fold_in(key_of[3], 71), 0),
        "start": bell_draw(key_of[2], (SLICES * N, N), 1.0, 6.0, ((0, 256),), jnp.float32),
    }


DTAU = 0.0625
LAMBDA = 0.5
EPS = 1e-06

def build_hop(neighbours):
    labels = jnp.arange(N, dtype=jnp.int32)
    kmat = jnp.zeros((N, N), jnp.float32)
    for k in range(4):
        kmat = kmat + (neighbours[:, k][:, None] == labels[None, :]).astype(jnp.float32)
    ksq = jnp.dot(kmat, kmat, precision=lax.Precision.HIGHEST)
    eye = jnp.eye(N, dtype=jnp.float32)
    return (eye + DTAU * kmat + 0.5 * DTAU * DTAU * ksq).astype(jnp.bfloat16)

def apply_all(stack, hop, factor):
    prod = jnp.einsum('lij,jk->lik', stack.astype(jnp.float32), hop.astype(jnp.float32), precision=lax.Precision.HIGHEST)
    return (prod * factor[:, None, :]).astype(jnp.bfloat16)

def reference(spins, neighbours, start):
    hop = build_hop(neighbours)
    factor = jnp.exp(LAMBDA * spins.astype(jnp.float32))
    single = (hop.astype(jnp.float32)[None, :, :] * factor[:, None, :]).astype(jnp.bfloat16)
    pair = apply_all(jnp.roll(single, 1, axis=0), hop, factor)
    triple = apply_all(jnp.roll(pair, 1, axis=0), hop, factor)
    block = apply_all(jnp.roll(triple, 1, axis=0), hop, factor)
    current = start.reshape(SLICES, N, N)
    sign = jnp.where(jnp.arange(SLICES) < 4, -1.0, 1.0).astype(jnp.float32)
    logsum = jnp.zeros((SLICES, N), jnp.float32)
    for step in range(STEPS):
        rounded = jnp.roll(current.astype(jnp.bfloat16), 4, axis=0)
        image = jnp.einsum('lij,ljk->lik', rounded.astype(jnp.float32), block.astype(jnp.float32), precision=lax.Precision.HIGHEST)
        image = image * sign[:, None, None]
        rms = jnp.sqrt(lax.optimization_barrier(jnp.mean(image * image, axis=2)) + EPS)
        current = image / rms[:, :, None]
        logsum = logsum + jnp.log(rms)
    return (current.reshape(SLICES * N, N), (logsum / (4.0 * STEPS)).reshape(SLICES * N))
```

```python
import functools

import jax
import jax.numpy as jnp
from jax import lax
from jax.experimental import pallas as pl
from jax.experimental.pallas import tpu as pltpu
from jax.sharding import PartitionSpec as P

STEPS = 4
SPAN = 4

DTAU = 0.0625
LAMBDA = 0.5
EPS = 1e-06

VMEM = pl.BlockSpec(memory_space=pltpu.VMEM)
SMEM = pl.BlockSpec(memory_space=pltpu.SMEM)


def from_behind(value, axis, by):
    length = lax.axis_size(axis)
    return lax.ppermute(value, axis, [(i, (i + by) % length) for i in range(length)])


def hop_kernel(band, table_ref, hop_ref, k_ref):
    sites = table_ref.shape[1]
    rows = [jnp.broadcast_to(table_ref[k : k + 1, :], (band, sites)) for k in range(4)]
    label = lax.broadcasted_iota(jnp.int32, (band, sites), 0)
    column = lax.broadcasted_iota(jnp.int32, (band, sites), 1)
    for b in range(sites // band):
        own = slice(b * band, (b + 1) * band)
        hits = jnp.zeros((band, sites), jnp.float32)
        for k in range(4):
            hits = hits + jnp.where(rows[k] == label + b * band, 1.0, 0.0)
        k_ref[own, :] = hits.astype(k_ref.dtype)
    for b in range(sites // band):
        own = slice(b * band, (b + 1) * band)
        ksq = jnp.dot(k_ref[own, :], k_ref[...], preferred_element_type=jnp.float32)
        eye = jnp.where(column == label + b * band, 1.0, 0.0)
        hop_ref[own, :] = (
            eye + DTAU * k_ref[own, :].astype(jnp.float32) + 0.5 * DTAU * DTAU * ksq
        ).astype(hop_ref.dtype)


def propagator(neighbours):
    sites = neighbours.shape[0]
    return pl.pallas_call(
        functools.partial(hop_kernel, 384),
        out_shape=jax.ShapeDtypeStruct((sites, sites), jnp.bfloat16),
        in_specs=[VMEM],
        out_specs=VMEM,
        scratch_shapes=[pltpu.VMEM((sites, sites), jnp.float8_e4m3fn)],
        compiler_params=pltpu.CompilerParams(vmem_limit_bytes=40 << 20),
        name="hop",
    )(neighbours.T)


def steps_kernel(last, x_ref, hop_ref, *refs):
    spin_refs, rest = (refs[:1], refs[1:]) if last else (refs[: STEPS - 1], refs[STEPS - 1 :])
    sign_ref, rest = (rest[0], rest[1:]) if last else (None, rest)
    out_ref, log_refs = rest[0], rest[1:]
    current = x_ref[...]
    for spin_ref, log_ref in zip(spin_refs, log_refs):
        factor = jnp.exp(LAMBDA * spin_ref[...].astype(jnp.float32))
        for part in range(SPAN):
            image = jnp.dot(current, hop_ref[...], preferred_element_type=jnp.float32)
            image = image * factor[part : part + 1, :]
            if part < SPAN - 1:
                current = image.astype(jnp.bfloat16)
        rms = jnp.sqrt(jnp.mean(image * image, axis=1, keepdims=True) + EPS)
        image = image / rms
        current = image.astype(jnp.bfloat16)
        wide = jnp.broadcast_to(jnp.log(rms) / (STEPS * SPAN), (rms.shape[0], 128))
        log_ref[...] = wide.T[0:1, :]
    out_ref[...] = image * sign_ref[0] if last else current


def steps(x, hop, groups, sign=None):
    rows, sites = x.shape
    last = sign is not None
    return pl.pallas_call(
        functools.partial(steps_kernel, last),
        out_shape=[jax.ShapeDtypeStruct((rows, sites), jnp.float32 if last else jnp.bfloat16)]
        + [jax.ShapeDtypeStruct((1, rows), jnp.float32)] * len(groups),
        in_specs=[VMEM] * (2 + len(groups)) + [SMEM] * last,
        out_specs=[VMEM] * (1 + len(groups)),
        compiler_params=pltpu.CompilerParams(vmem_limit_bytes=40 << 20),
        name="last_step" if last else "first_steps",
    )(x, hop, *groups, *([sign] if last else []))


def shards(spins, neighbours, start):
    row = spins.astype(jnp.bfloat16)
    four = jnp.concatenate([from_behind(row, "tm", by) for by in (3, 2, 1)] + [row], axis=0)
    groups = [from_behind(four, "tm", by) for by in (12, 8, 4)] + [four]
    incoming = from_behind(start.astype(jnp.bfloat16), "tm", STEPS * SPAN)
    hop = propagator(neighbours)
    sign = jnp.where(lax.axis_index("tm") < STEPS * SPAN, -1.0, 1.0).astype(jnp.float32)
    current, *logs = steps(incoming, hop, groups[:-1])
    logs = [from_behind(log, "tm", -SPAN * (STEPS - 1 - t)) for t, log in enumerate(logs)]
    panels, growth = steps(current, hop, groups[-1:], sign[None])
    for log in logs:
        growth = growth + log
    return panels, growth[0]


def solution(mesh):
    return jax.shard_map(
        shards,
        mesh=mesh,
        in_specs=(P("tm", None), P(), P(("tm", "panel"), None)),
        out_specs=(P(("tm", "panel"), None), P(("tm", "panel"))),
        check_vma=False,
    )
```

```python
import functools

import jax
import jax.numpy as jnp
from jax import lax
from jax.experimental import pallas as pl
from jax.experimental.pallas import tpu as pltpu
from jax.sharding import PartitionSpec as P

STEPS = 4
SPAN = 4

DTAU = 0.0625
LAMBDA = 0.5
EPS = 1e-06

VMEM = pl.BlockSpec(memory_space=pltpu.VMEM)
SMEM = pl.BlockSpec(memory_space=pltpu.SMEM)


def from_behind(value, axis, by):
    length = lax.axis_size(axis)
    return lax.ppermute(value, axis, [(i, (i + by) % length) for i in range(length)])


def hop_kernel(band, table_ref, hop_ref, k_ref):
    sites = table_ref.shape[1]
    rows = [jnp.broadcast_to(table_ref[k : k + 1, :], (band, sites)) for k in range(4)]
    label = lax.broadcasted_iota(jnp.int32, (band, sites), 0)
    column = lax.broadcasted_iota(jnp.int32, (band, sites), 1)
    for b in range(sites // band):
        own = slice(b * band, (b + 1) * band)
        hits = jnp.zeros((band, sites), jnp.float32)
        for k in range(4):
            hits = hits + jnp.where(rows[k] == label + b * band, 1.0, 0.0)
        k_ref[own, :] = hits.astype(k_ref.dtype)
    for b in range(sites // band):
        own = slice(b * band, (b + 1) * band)
        ksq = jnp.dot(k_ref[own, :], k_ref[...], preferred_element_type=jnp.float32)
        eye = jnp.where(column == label + b * band, 1.0, 0.0)
        hop_ref[own, :] = (
            eye + DTAU * k_ref[own, :].astype(jnp.float32) + 0.5 * DTAU * DTAU * ksq
        ).astype(hop_ref.dtype)


def propagator(neighbours):
    sites = neighbours.shape[0]
    return pl.pallas_call(
        functools.partial(hop_kernel, 384),
        out_shape=jax.ShapeDtypeStruct((sites, sites), jnp.bfloat16),
        in_specs=[VMEM],
        out_specs=VMEM,
        scratch_shapes=[pltpu.VMEM((sites, sites), jnp.float8_e4m3fn)],
        compiler_params=pltpu.CompilerParams(vmem_limit_bytes=40 << 20),
        name="hop",
    )(neighbours.T)


def steps_kernel(first, count, place_ref, x_ref, hop_ref, spins_ref, out_ref, logs_ref, factor_ref):
    last = first + count == STEPS
    slices = spins_ref.shape[0]
    factor_ref[...] = jnp.exp(LAMBDA * spins_ref[...].astype(jnp.float32))
    place = place_ref[0]
    current = x_ref[...]
    logs = []
    for step in range(first, first + count):
        for part in range(SPAN):
            back = STEPS * SPAN - 1 - (step * SPAN + part)
            row = lax.rem(place + (slices - back), slices)
            image = jnp.dot(current, hop_ref[...], preferred_element_type=jnp.float32)
            image = image * factor_ref[pl.ds(row, 1), :]
            if part < SPAN - 1:
                current = image.astype(jnp.bfloat16)
        rms = jnp.sqrt(jnp.mean(image * image, axis=1, keepdims=True) + EPS)
        image = image / rms
        current = image.astype(jnp.bfloat16)
        wide = jnp.broadcast_to(jnp.log(rms) / (STEPS * SPAN), (rms.shape[0], 128))
        logs.append(wide.T[0:1, :])
    for i, log in enumerate(logs):
        logs_ref[i : i + 1, :] = log
    if last:
        image = image * jnp.where(place < STEPS * SPAN, -1.0, 1.0)
    out_ref[...] = image if last else current


def steps(first, count, place, x, hop, spins):
    rows, sites = x.shape
    last = first + count == STEPS
    return pl.pallas_call(
        functools.partial(steps_kernel, first, count),
        out_shape=[
            jax.ShapeDtypeStruct((rows, sites), jnp.float32 if last else jnp.bfloat16),
            jax.ShapeDtypeStruct((count, rows), jnp.float32),
        ],
        in_specs=[SMEM, VMEM, VMEM, VMEM],
        out_specs=[VMEM, VMEM],
        scratch_shapes=[pltpu.VMEM(spins.shape, jnp.float32)],
        compiler_params=pltpu.CompilerParams(vmem_limit_bytes=40 << 20),
        name=f"steps_{first}",
    )(place, x, hop, spins)


def shards(spins, neighbours, start):
    every = lax.all_gather(spins.astype(jnp.bfloat16), "tm", axis=0, tiled=True)
    incoming = from_behind(start.astype(jnp.bfloat16), "tm", STEPS * SPAN)
    hop = propagator(neighbours)
    place = lax.axis_index("tm")[None]
    x, logs = steps(0, 2, place, incoming, hop, every)
    early = from_behind(logs, "tm", -2 * SPAN)
    x, late = steps(2, 1, place, x, hop, every)
    late = from_behind(jnp.concatenate([late, early[:1]], axis=0), "tm", -SPAN)
    panels, growth = steps(3, 1, place, x, hop, every)
    growth = growth[0] + late[0] + late[1] + early[1]
    return panels, growth


def solution(mesh):
    return jax.shard_map(
        shards,
        mesh=mesh,
        in_specs=(P("tm", None), P(), P(("tm", "panel"), None)),
        out_specs=(P(("tm", "panel"), None), P(("tm", "panel"))),
        check_vma=False,
    )
```

```python
import functools

import jax
import jax.numpy as jnp
from jax import lax
from jax.experimental import pallas as pl
from jax.experimental.pallas import tpu as pltpu
from jax.sharding import PartitionSpec as P

STEPS = 4
SPAN = 4

DTAU = 0.0625
LAMBDA = 0.5
EPS = 1e-06

VMEM = pl.BlockSpec(memory_space=pltpu.VMEM)
SMEM = pl.BlockSpec(memory_space=pltpu.SMEM)


def from_behind(value, axis, by):
    length = lax.axis_size(axis)
    return lax.ppermute(value, axis, [(i, (i + by) % length) for i in range(length)])


def hop_kernel(band, table_ref, hop_ref, k_ref):
    sites = table_ref.shape[1]
    rows = [jnp.broadcast_to(table_ref[k : k + 1, :], (band, sites)) for k in range(4)]
    label = lax.broadcasted_iota(jnp.int32, (band, sites), 0)
    column = lax.broadcasted_iota(jnp.int32, (band, sites), 1)
    for b in range(sites // band):
        own = slice(b * band, (b + 1) * band)
        hits = jnp.zeros((band, sites), jnp.float32)
        for k in range(4):
            hits = hits + jnp.where(rows[k] == label + b * band, 1.0, 0.0)
        k_ref[own, :] = hits.astype(k_ref.dtype)
    for b in range(sites // band):
        own = slice(b * band, (b + 1) * band)
        ksq = jnp.dot(k_ref[own, :], k_ref[...], preferred_element_type=jnp.float32)
        eye = jnp.where(column == label + b * band, 1.0, 0.0)
        hop_ref[own, :] = (
            eye + DTAU * k_ref[own, :].astype(jnp.float32) + 0.5 * DTAU * DTAU * ksq
        ).astype(hop_ref.dtype)


def propagator(neighbours):
    sites = neighbours.shape[0]
    return pl.pallas_call(
        functools.partial(hop_kernel, 384),
        out_shape=jax.ShapeDtypeStruct((sites, sites), jnp.bfloat16),
        in_specs=[VMEM],
        out_specs=VMEM,
        scratch_shapes=[pltpu.VMEM((sites, sites), jnp.float8_e4m3fn)],
        compiler_params=pltpu.CompilerParams(vmem_limit_bytes=40 << 20),
        name="hop",
    )(neighbours.T)


def step_kernel(last, place_ref, x_ref, hop_ref, spins_ref, out_ref, log_ref):
    factor = jnp.exp(LAMBDA * spins_ref[...].astype(jnp.float32))
    current = x_ref[...]
    for part in range(SPAN):
        image = jnp.dot(current, hop_ref[...], preferred_element_type=jnp.float32)
        image = image * factor[part : part + 1, :]
        if part < SPAN - 1:
            current = image.astype(jnp.bfloat16)
    rms = jnp.sqrt(jnp.mean(image * image, axis=1, keepdims=True) + EPS)
    image = image / rms
    wide = jnp.broadcast_to(jnp.log(rms) / (STEPS * SPAN), (rms.shape[0], 128))
    log_ref[...] = wide.T[0:1, :]
    if last:
        image = image * jnp.where(place_ref[0] < STEPS * SPAN, -1.0, 1.0)
    out_ref[...] = image.astype(out_ref.dtype)


def step(number, place, x, hop, group):
    rows, sites = x.shape
    last = number == STEPS - 1
    return pl.pallas_call(
        functools.partial(step_kernel, last),
        out_shape=[
            jax.ShapeDtypeStruct((rows, sites), jnp.float32 if last else jnp.bfloat16),
            jax.ShapeDtypeStruct((1, rows), jnp.float32),
        ],
        in_specs=[SMEM, VMEM, VMEM, VMEM],
        out_specs=[VMEM, VMEM],
        compiler_params=pltpu.CompilerParams(vmem_limit_bytes=40 << 20),
        name=f"step_{number}",
    )(place, x, hop, group)


def shards(spins, neighbours, start):
    place = lax.axis_index("tm")[None]
    incoming = from_behind(start.astype(jnp.bfloat16), "tm", STEPS * SPAN)
    row = spins.astype(jnp.bfloat16)
    parts = [from_behind(row, "tm", by) for by in (15, 14, 13, 12)]
    hop = propagator(neighbours)
    parts, hop = lax.optimization_barrier((parts, hop))
    group0 = jnp.concatenate(parts, axis=0)
    group1 = from_behind(group0, "tm", -SPAN)
    x, log0 = step(0, place, incoming, hop, group0)
    group1, x = lax.optimization_barrier((group1, x))
    both = from_behind(jnp.concatenate([group0, group1], axis=0), "tm", -2 * SPAN)
    x, log1 = step(1, place, x, hop, group1)
    early = from_behind(jnp.concatenate([log0, log1], axis=0), "tm", -2 * SPAN)
    x, log2 = step(2, place, x, hop, both[:SPAN])
    late = from_behind(jnp.concatenate([log2, early[:1]], axis=0), "tm", -SPAN)
    panels, log3 = step(3, place, x, hop, both[SPAN:])
    growth = log3[0] + late[0] + late[1] + early[1]
    return panels, growth


def solution(mesh):
    return jax.shard_map(
        shards,
        mesh=mesh,
        in_specs=(P("tm", None), P(), P(("tm", "panel"), None)),
        out_specs=(P(("tm", "panel"), None), P(("tm", "panel"))),
        check_vma=False,
    )
```

```python
import functools

import jax
import jax.numpy as jnp
from jax import lax
from jax.experimental import pallas as pl
from jax.experimental.pallas import tpu as pltpu
from jax.sharding import PartitionSpec as P

STEPS = 4
SPAN = 4

DTAU = 0.0625
LAMBDA = 0.5
EPS = 1e-06

VMEM = pl.BlockSpec(memory_space=pltpu.VMEM)
SMEM = pl.BlockSpec(memory_space=pltpu.SMEM)


def from_behind(value, axis, by):
    length = lax.axis_size(axis)
    return lax.ppermute(value, axis, [(i, (i + by) % length) for i in range(length)])


def hop_kernel(band, table_ref, hop_ref, k_ref):
    sites = table_ref.shape[1]
    rows = [jnp.broadcast_to(table_ref[k : k + 1, :], (band, sites)) for k in range(4)]
    label = lax.broadcasted_iota(jnp.int32, (band, sites), 0)
    column = lax.broadcasted_iota(jnp.int32, (band, sites), 1)
    for b in range(sites // band):
        own = slice(b * band, (b + 1) * band)
        hits = jnp.zeros((band, sites), jnp.float32)
        for k in range(4):
            hits = hits + jnp.where(rows[k] == label + b * band, 1.0, 0.0)
        k_ref[own, :] = hits.astype(k_ref.dtype)
    for b in range(sites // band):
        own = slice(b * band, (b + 1) * band)
        ksq = jnp.dot(k_ref[own, :], k_ref[...], preferred_element_type=jnp.float32)
        eye = jnp.where(column == label + b * band, 1.0, 0.0)
        hop_ref[own, :] = (
            eye + DTAU * k_ref[own, :].astype(jnp.float32) + 0.5 * DTAU * DTAU * ksq
        ).astype(hop_ref.dtype)


def propagator(neighbours):
    sites = neighbours.shape[0]
    return pl.pallas_call(
        functools.partial(hop_kernel, 384),
        out_shape=jax.ShapeDtypeStruct((sites, sites), jnp.bfloat16),
        in_specs=[VMEM],
        out_specs=VMEM,
        scratch_shapes=[pltpu.VMEM((sites, sites), jnp.float8_e4m3fn)],
        compiler_params=pltpu.CompilerParams(vmem_limit_bytes=16 << 20),
        name="hop",
    )(neighbours.T)


def step_kernel(last, place_ref, x_ref, hop_ref, spins_ref, out_ref, log_ref):
    factor = jnp.exp(LAMBDA * spins_ref[...].astype(jnp.float32))
    current = x_ref[...]
    for part in range(SPAN):
        image = jnp.dot(current, hop_ref[...], preferred_element_type=jnp.float32)
        image = image * factor[part : part + 1, :]
        if part < SPAN - 1:
            current = image.astype(jnp.bfloat16)
    rms = jnp.sqrt(jnp.mean(image * image, axis=1, keepdims=True) + EPS)
    image = image / rms
    wide = jnp.broadcast_to(jnp.log(rms) / (STEPS * SPAN), (rms.shape[0], 128))
    log_ref[...] = wide.T[0:1, :]
    if last:
        image = image * jnp.where(place_ref[0] < STEPS * SPAN, -1.0, 1.0)
    out_ref[...] = image.astype(out_ref.dtype)


def step(number, place, x, hop, group):
    rows, sites = x.shape
    last = number == STEPS - 1
    return pl.pallas_call(
        functools.partial(step_kernel, last),
        out_shape=[
            jax.ShapeDtypeStruct((rows, sites), jnp.float32 if last else jnp.bfloat16),
            jax.ShapeDtypeStruct((1, rows), jnp.float32),
        ],
        in_specs=[SMEM, VMEM, VMEM, VMEM],
        out_specs=[VMEM, VMEM],
        compiler_params=pltpu.CompilerParams(vmem_limit_bytes=16 << 20),
        name=f"step_{number}",
    )(place, x, hop, group)


def shards(spins, neighbours, start):
    place = lax.axis_index("tm")[None]
    incoming = from_behind(start.astype(jnp.bfloat16), "tm", STEPS * SPAN)
    row = spins.astype(jnp.bfloat16)
    near = [from_behind(row, "tm", by) for by in (3, 2, 1)]
    hop = propagator(neighbours)
    near, hop = lax.optimization_barrier((near, hop))
    own = jnp.concatenate(near + [row], axis=0)
    groups = [from_behind(own, "tm", SPAN * (STEPS - 1 - t)) for t in range(STEPS - 1)] + [own]
    x, log0 = step(0, place, incoming, hop, groups[0])
    groups[1], x = lax.optimization_barrier((groups[1], x))
    x, log1 = step(1, place, x, hop, groups[1])
    early = from_behind(jnp.concatenate([log0, log1], axis=0), "tm", -2 * SPAN)
    groups[2], x = lax.optimization_barrier((groups[2], x))
    x, log2 = step(2, place, x, hop, groups[2])
    early, log2 = lax.optimization_barrier((early, log2))
    late = from_behind(jnp.concatenate([log2, early[:1]], axis=0), "tm", -SPAN)
    panels, log3 = step(3, place, x, hop, groups[3])
    growth = log3[0] + late[0] + late[1] + early[1]
    return panels, growth


def solution(mesh):
    return jax.shard_map(
        shards,
        mesh=mesh,
        in_specs=(P("tm", None), P(), P(("tm", "panel"), None)),
        out_specs=(P(("tm", "panel"), None), P(("tm", "panel"))),
        check_vma=False,
    )
```

```python
import functools

import jax
import jax.numpy as jnp
from jax import lax
from jax.experimental import pallas as pl
from jax.experimental.pallas import tpu as pltpu
from jax.sharding import PartitionSpec as P

STEPS = 4
SPAN = 4

DTAU = 0.0625
LAMBDA = 0.5
EPS = 1e-06

VMEM = pl.BlockSpec(memory_space=pltpu.VMEM)
SMEM = pl.BlockSpec(memory_space=pltpu.SMEM)


def from_behind(value, axis, by):
    length = lax.axis_size(axis)
    return lax.ppermute(value, axis, [(i, (i + by) % length) for i in range(length)])


def hopping_kernel(band, table_ref, k_ref):
    sites = table_ref.shape[1]
    rows = [jnp.broadcast_to(table_ref[k : k + 1, :], (band, sites)) for k in range(4)]
    label = lax.broadcasted_iota(jnp.int32, (band, sites), 0)
    for b in range(sites // band):
        hits = jnp.zeros((band, sites), jnp.float32)
        for k in range(4):
            hits = hits + jnp.where(rows[k] == label + b * band, 1.0, 0.0)
        k_ref[b * band : (b + 1) * band, :] = hits.astype(k_ref.dtype)


def hop_kernel(band, k_ref, hop_ref):
    sites = k_ref.shape[0]
    label = lax.broadcasted_iota(jnp.int32, (band, sites), 0)
    column = lax.broadcasted_iota(jnp.int32, (band, sites), 1)
    for b in range(sites // band):
        own = slice(b * band, (b + 1) * band)
        ksq = jnp.dot(k_ref[own, :], k_ref[...], preferred_element_type=jnp.float32)
        eye = jnp.where(column == label + b * band, 1.0, 0.0)
        hop_ref[own, :] = (
            eye + DTAU * k_ref[own, :].astype(jnp.float32) + 0.5 * DTAU * DTAU * ksq
        ).astype(hop_ref.dtype)


def square_kernel(kernel, name, operand, dtype):
    sites = operand.shape[1]
    return pl.pallas_call(
        functools.partial(kernel, 384),
        out_shape=jax.ShapeDtypeStruct((sites, sites), dtype),
        in_specs=[VMEM],
        out_specs=VMEM,
        compiler_params=pltpu.CompilerParams(vmem_limit_bytes=16 << 20),
        name=name,
    )(operand)


def step_kernel(last, place_ref, x_ref, hop_ref, spins_ref, out_ref, log_ref):
    factor = jnp.exp(LAMBDA * spins_ref[...].astype(jnp.float32))
    current = x_ref[...]
    for part in range(SPAN):
        image = jnp.dot(current, hop_ref[...], preferred_element_type=jnp.float32)
        image = image * factor[part : part + 1, :]
        if part < SPAN - 1:
            current = image.astype(jnp.bfloat16)
    rms = jnp.sqrt(jnp.mean(image * image, axis=1, keepdims=True) + EPS)
    image = image / rms
    wide = jnp.broadcast_to(jnp.log(rms) / (STEPS * SPAN), (rms.shape[0], 128))
    log_ref[...] = wide.T[0:1, :]
    if last:
        image = image * jnp.where(place_ref[0] < STEPS * SPAN, -1.0, 1.0)
    out_ref[...] = image.astype(out_ref.dtype)


def step(number, place, x, hop, group):
    rows, sites = x.shape
    last = number == STEPS - 1
    return pl.pallas_call(
        functools.partial(step_kernel, last),
        out_shape=[
            jax.ShapeDtypeStruct((rows, sites), jnp.float32 if last else jnp.bfloat16),
            jax.ShapeDtypeStruct((1, rows), jnp.float32),
        ],
        in_specs=[SMEM, VMEM, VMEM, VMEM],
        out_specs=[VMEM, VMEM],
        compiler_params=pltpu.CompilerParams(vmem_limit_bytes=16 << 20),
        name=f"step_{number}",
    )(place, x, hop, group)


def shards(spins, neighbours, start):
    place = lax.axis_index("tm")[None]
    incoming = from_behind(start.astype(jnp.bfloat16), "tm", STEPS * SPAN)
    row = spins.astype(jnp.bfloat16)
    near = [from_behind(row, "tm", by) for by in (3, 2, 1)]
    hopping = square_kernel(hopping_kernel, "hopping", neighbours.T, jnp.float8_e4m3fn)
    near, hopping = lax.optimization_barrier((near, hopping))
    own = jnp.concatenate(near + [row], axis=0)
    group0 = from_behind(own, "tm", 3 * SPAN)
    group1 = from_behind(own, "tm", 2 * SPAN)
    own, hopping = lax.optimization_barrier((own, hopping))
    hop = square_kernel(hop_kernel, "hop", hopping, jnp.bfloat16)
    group0, group1, hop = lax.optimization_barrier((group0, group1, hop))
    x, log0 = step(0, place, incoming, hop, group0)
    pad = ((0, 0), (0, group0.shape[1] - log0.shape[1]))
    sent = jnp.concatenate([group0.astype(jnp.float32), jnp.pad(log0, pad)], axis=0)
    came = from_behind(sent, "tm", -2 * SPAN)
    group1, x = lax.optimization_barrier((group1, x))
    x, log1 = step(1, place, x, hop, group1)
    middle = from_behind(log1, "tm", -2 * SPAN)
    came, x = lax.optimization_barrier((came, x))
    x, log2 = step(2, place, x, hop, came[:SPAN])
    late = from_behind(jnp.concatenate([log2, came[SPAN:, : log2.shape[1]]], axis=0), "tm", -SPAN)
    panels, log3 = step(3, place, x, hop, own)
    growth = log3[0] + late[0] + late[1] + middle[0]
    return panels, growth


def solution(mesh):
    return jax.shard_map(
        shards,
        mesh=mesh,
        in_specs=(P("tm", None), P(), P(("tm", "panel"), None)),
        out_specs=(P(("tm", "panel"), None), P(("tm", "panel"))),
        check_vma=False,
    )
```

```python
import functools

import jax
import jax.numpy as jnp
from jax import lax
from jax.experimental import pallas as pl
from jax.experimental.pallas import tpu as pltpu
from jax.sharding import PartitionSpec as P

STEPS = 4
SPAN = 4

DTAU = 0.0625
LAMBDA = 0.5
EPS = 1e-06

VMEM = pl.BlockSpec(memory_space=pltpu.VMEM)
SMEM = pl.BlockSpec(memory_space=pltpu.SMEM)


def from_behind(value, axis, by):
    length = lax.axis_size(axis)
    return lax.ppermute(value, axis, [(i, (i + by) % length) for i in range(length)])


def hopping_kernel(band, table_ref, k_ref):
    sites = table_ref.shape[1]
    rows = [jnp.broadcast_to(table_ref[k : k + 1, :], (band, sites)) for k in range(4)]
    label = lax.broadcasted_iota(jnp.int32, (band, sites), 0)
    for b in range(sites // band):
        hits = jnp.zeros((band, sites), jnp.float32)
        for k in range(4):
            hits = hits + jnp.where(rows[k] == label + b * band, 1.0, 0.0)
        k_ref[b * band : (b + 1) * band, :] = hits.astype(k_ref.dtype)


def hop_kernel(band, k_ref, hop_ref):
    sites = k_ref.shape[0]
    label = lax.broadcasted_iota(jnp.int32, (band, sites), 0)
    column = lax.broadcasted_iota(jnp.int32, (band, sites), 1)
    for b in range(sites // band):
        own = slice(b * band, (b + 1) * band)
        ksq = jnp.dot(k_ref[own, :], k_ref[...], preferred_element_type=jnp.float32)
        eye = jnp.where(column == label + b * band, 1.0, 0.0)
        hop_ref[own, :] = (
            eye + DTAU * k_ref[own, :].astype(jnp.float32) + 0.5 * DTAU * DTAU * ksq
        ).astype(hop_ref.dtype)


def square_kernel(kernel, name, operand, dtype):
    sites = operand.shape[1]
    return pl.pallas_call(
        functools.partial(kernel, 384),
        out_shape=jax.ShapeDtypeStruct((sites, sites), dtype),
        in_specs=[VMEM],
        out_specs=VMEM,
        compiler_params=pltpu.CompilerParams(vmem_limit_bytes=16 << 20),
        name=name,
    )(operand)


def step_kernel(x_ref, hop_ref, spins_ref, out_ref, log_ref):
    factor = jnp.exp(LAMBDA * spins_ref[...].astype(jnp.float32))
    image = passed(x_ref[...], hop_ref, factor, 0)
    image, log = normalized(image)
    log_ref[...] = log.T[0:1, :]
    out_ref[...] = image.astype(out_ref.dtype)


def last_kernel(place_ref, x_ref, hop_ref, spins_ref, out_ref, log_ref, half_ref, sem):
    sign = jnp.where(place_ref[0] < STEPS * SPAN, -1.0, 1.0)
    factor = jnp.exp(LAMBDA * spins_ref[...].astype(jnp.float32))
    current = passed(x_ref[...], hop_ref, factor, 1).astype(jnp.bfloat16)
    rows = current.shape[0] // 2
    copies, logs = [], []
    for h in range(2):
        image = jnp.dot(current[h * rows : (h + 1) * rows], hop_ref[...], preferred_element_type=jnp.float32)
        image, log = normalized(image * factor[SPAN - 1 : SPAN, :])
        half_ref[h] = image * sign
        copies.append(pltpu.make_async_copy(half_ref.at[h], out_ref.at[pl.ds(h * rows, rows)], sem.at[h]))
        copies[h].start()
        logs.append(log)
    log_ref[...] = jnp.concatenate(logs, axis=0).T[0:1, :]
    for copy in copies:
        copy.wait()


def passed(current, hop_ref, factor, left):
    for part in range(SPAN - left):
        image = jnp.dot(current, hop_ref[...], preferred_element_type=jnp.float32)
        image = image * factor[part : part + 1, :]
        current = image.astype(jnp.bfloat16)
    return image


def normalized(image):
    rms = jnp.sqrt(jnp.mean(image * image, axis=1, keepdims=True) + EPS)
    log = jnp.broadcast_to(jnp.log(rms) / (STEPS * SPAN), (rms.shape[0], 128))
    return image * (1.0 / rms), log


def step(number, place, x, hop, group):
    rows, sites = x.shape
    last = number == STEPS - 1
    return pl.pallas_call(
        last_kernel if last else step_kernel,
        out_shape=[
            jax.ShapeDtypeStruct((rows, sites), jnp.float32 if last else jnp.bfloat16),
            jax.ShapeDtypeStruct((1, rows), jnp.float32),
        ],
        in_specs=[SMEM] * last + [VMEM] * 3,
        out_specs=[pl.BlockSpec(memory_space=pl.ANY) if last else VMEM, VMEM],
        scratch_shapes=[pltpu.VMEM((2, rows // 2, sites), jnp.float32), pltpu.SemaphoreType.DMA((2,))] if last else [],
        compiler_params=pltpu.CompilerParams(vmem_limit_bytes=16 << 20),
        name=f"step_{number}",
    )(*([place] if last else []), x, hop, group)


def shards(spins, neighbours, start):
    place = lax.axis_index("tm")[None]
    incoming = from_behind(start.astype(jnp.bfloat16), "tm", STEPS * SPAN)
    row = spins.astype(jnp.bfloat16)
    near = [from_behind(row, "tm", by) for by in (3, 2, 1)]
    own = jnp.concatenate(near + [row], axis=0)
    group0 = from_behind(own, "tm", 3 * SPAN)
    group1 = from_behind(own, "tm", 2 * SPAN)
    own, table = lax.optimization_barrier((own, neighbours.T))
    hopping = square_kernel(hopping_kernel, "hopping", table, jnp.float8_e4m3fn)
    hop = square_kernel(hop_kernel, "hop", hopping, jnp.bfloat16)
    group0, group1, hop = lax.optimization_barrier((group0, group1, hop))
    group2 = from_behind(group0, "tm", -2 * SPAN)
    x, log0 = step(0, place, incoming, hop, group0)
    group1, x = lax.optimization_barrier((group1, x))
    x, log1 = step(1, place, x, hop, group1)
    early = from_behind(jnp.concatenate([log0, log1], axis=0), "tm", -2 * SPAN)
    group2, x = lax.optimization_barrier((group2, x))
    x, log2 = step(2, place, x, hop, group2)
    early, log2 = lax.optimization_barrier((early, log2))
    late = from_behind(jnp.concatenate([log2, early[:1]], axis=0), "tm", -SPAN)
    panels, log3 = step(3, place, x, hop, own)
    growth = log3[0] + late[0] + late[1] + early[1]
    return panels, growth


def solution(mesh):
    return jax.shard_map(
        shards,
        mesh=mesh,
        in_specs=(P("tm", None), P(), P(("tm", "panel"), None)),
        out_specs=(P(("tm", "panel"), None), P(("tm", "panel"))),
        check_vma=False,
    )
```

```python
import functools

import jax
import jax.numpy as jnp
from jax import lax
from jax.experimental import pallas as pl
from jax.experimental.pallas import tpu as pltpu
from jax.sharding import PartitionSpec as P

STEPS = 4
SPAN = 4

DTAU = 0.0625
LAMBDA = 0.5
EPS = 1e-06

VMEM = pl.BlockSpec(memory_space=pltpu.VMEM)
SMEM = pl.BlockSpec(memory_space=pltpu.SMEM)


def from_behind(value, axis, by):
    length = lax.axis_size(axis)
    return lax.ppermute(value, axis, [(i, (i + by) % length) for i in range(length)])


def hopping_kernel(band, table_ref, k_ref):
    sites = table_ref.shape[1]
    rows = [jnp.broadcast_to(table_ref[k : k + 1, :], (band, sites)) for k in range(4)]
    label = lax.broadcasted_iota(jnp.int32, (band, sites), 0)
    for b in range(sites // band):
        hits = jnp.zeros((band, sites), jnp.float32)
        for k in range(4):
            hits = hits + jnp.where(rows[k] == label + b * band, 1.0, 0.0)
        k_ref[b * band : (b + 1) * band, :] = hits.astype(k_ref.dtype)


def hop_kernel(band, k_ref, hop_ref):
    sites = k_ref.shape[0]
    label = lax.broadcasted_iota(jnp.int32, (band, sites), 0)
    column = lax.broadcasted_iota(jnp.int32, (band, sites), 1)
    for b in range(sites // band):
        own = slice(b * band, (b + 1) * band)
        ksq = jnp.dot(k_ref[own, :], k_ref[...], preferred_element_type=jnp.float32)
        eye = jnp.where(column == label + b * band, 1.0, 0.0)
        hop_ref[own, :] = (
            eye + DTAU * k_ref[own, :].astype(jnp.float32) + 0.5 * DTAU * DTAU * ksq
        ).astype(hop_ref.dtype)


def square_kernel(kernel, name, operand, dtype):
    sites = operand.shape[1]
    return pl.pallas_call(
        functools.partial(kernel, 384),
        out_shape=jax.ShapeDtypeStruct((sites, sites), dtype),
        in_specs=[VMEM],
        out_specs=VMEM,
        compiler_params=pltpu.CompilerParams(vmem_limit_bytes=16 << 20),
        name=name,
    )(operand)


def lead_kernel(x_ref, hop_ref, out_ref):
    out_ref[...] = jnp.dot(x_ref[...], hop_ref[...], preferred_element_type=jnp.float32)


def step_kernel(first, x_ref, hop_ref, spins_ref, out_ref, log_ref):
    factor = jnp.exp(LAMBDA * spins_ref[...].astype(jnp.float32))
    current = x_ref[...]
    if first:
        current = (current * factor[:1, :]).astype(jnp.bfloat16)
    image = passed(current, hop_ref, factor, first, SPAN)
    image, log = normalized(image)
    log_ref[...] = log.T[0:1, :]
    out_ref[...] = image.astype(out_ref.dtype)


def last_kernel(place_ref, x_ref, hop_ref, spins_ref, out_ref, log_ref, half_ref, sem):
    sign = jnp.where(place_ref[0] < STEPS * SPAN, -1.0, 1.0)
    factor = jnp.exp(LAMBDA * spins_ref[...].astype(jnp.float32))
    current = passed(x_ref[...], hop_ref, factor, 0, SPAN - 1).astype(jnp.bfloat16)
    rows = current.shape[0] // 2
    copies, logs = [], []
    for h in range(2):
        image = jnp.dot(current[h * rows : (h + 1) * rows], hop_ref[...], preferred_element_type=jnp.float32)
        image, log = normalized(image * factor[SPAN - 1 : SPAN, :])
        half_ref[h] = image * sign
        copies.append(pltpu.make_async_copy(half_ref.at[h], out_ref.at[pl.ds(h * rows, rows)], sem.at[h]))
        copies[h].start()
        logs.append(log)
    log_ref[...] = jnp.concatenate(logs, axis=0).T[0:1, :]
    for copy in copies:
        copy.wait()


def passed(current, hop_ref, factor, begin, end):
    for part in range(begin, end):
        image = jnp.dot(current, hop_ref[...], preferred_element_type=jnp.float32)
        image = image * factor[part : part + 1, :]
        current = image.astype(jnp.bfloat16)
    return image


def normalized(image):
    rms = jnp.sqrt(jnp.mean(image * image, axis=1, keepdims=True) + EPS)
    log = jnp.broadcast_to(jnp.log(rms) / (STEPS * SPAN), (rms.shape[0], 128))
    return image * (1.0 / rms), log


def step(number, place, x, hop, group):
    rows, sites = x.shape
    last = number == STEPS - 1
    return pl.pallas_call(
        last_kernel if last else functools.partial(step_kernel, int(number == 0)),
        out_shape=[
            jax.ShapeDtypeStruct((rows, sites), jnp.float32 if last else jnp.bfloat16),
            jax.ShapeDtypeStruct((1, rows), jnp.float32),
        ],
        in_specs=[SMEM] * last + [VMEM] * 3,
        out_specs=[pl.BlockSpec(memory_space=pl.ANY) if last else VMEM, VMEM],
        scratch_shapes=[pltpu.VMEM((2, rows // 2, sites), jnp.float32), pltpu.SemaphoreType.DMA((2,))] if last else [],
        compiler_params=pltpu.CompilerParams(vmem_limit_bytes=16 << 20),
        name=f"step_{number}",
    )(*([place] if last else []), x, hop, group)


def lead(x, hop):
    return pl.pallas_call(
        lead_kernel,
        out_shape=jax.ShapeDtypeStruct(x.shape, jnp.float32),
        in_specs=[VMEM, VMEM],
        out_specs=VMEM,
        compiler_params=pltpu.CompilerParams(vmem_limit_bytes=16 << 20),
        name="lead",
    )(x, hop)


def shards(spins, neighbours, start):
    place = lax.axis_index("tm")[None]
    incoming = from_behind(start.astype(jnp.bfloat16), "tm", STEPS * SPAN)
    row = spins.astype(jnp.bfloat16)
    near = {by: from_behind(row, "tm", by) for by in (3, 2, 1)}
    near = [near[by] for by in (3, 2, 1)]
    hopping = square_kernel(hopping_kernel, "hopping", neighbours.T, jnp.float8_e4m3fn)
    near, hopping = lax.optimization_barrier((near, hopping))
    own = jnp.concatenate(near + [row], axis=0)
    group0 = from_behind(own, "tm", 3 * SPAN)
    group1 = from_behind(own, "tm", 2 * SPAN)
    own, hopping = lax.optimization_barrier((own, hopping))
    hop = square_kernel(hop_kernel, "hop", hopping, jnp.bfloat16)
    ahead = lead(incoming, hop)
    group0, ahead = lax.optimization_barrier((group0, ahead))
    x, log0 = step(0, place, ahead, hop, group0)
    group1, x = lax.optimization_barrier((group1, x))
    group0, x = lax.optimization_barrier((group0, x))
    group2 = from_behind(group0, "tm", -2 * SPAN)
    x, log1 = step(1, place, x, hop, group1)
    early = from_behind(jnp.concatenate([log0, log1], axis=0), "tm", -2 * SPAN)
    group2, x = lax.optimization_barrier((group2, x))
    x, log2 = step(2, place, x, hop, group2)
    early, log2 = lax.optimization_barrier((early, log2))
    early = [early[:1], early[1:]]
    late = from_behind(jnp.concatenate([log2, early[0]], axis=0), "tm", -SPAN)
    panels, log3 = step(3, place, x, hop, own)
    growth = log3[0] + late[0] + late[1] + early[1][0]
    return panels, growth


def solution(mesh):
    return jax.shard_map(
        shards,
        mesh=mesh,
        in_specs=(P("tm", None), P(), P(("tm", "panel"), None)),
        out_specs=(P(("tm", "panel"), None), P(("tm", "panel"))),
        check_vma=False,
    )
```

```python
import functools

import jax
import jax.numpy as jnp
from jax import lax
from jax.experimental import pallas as pl
from jax.experimental.pallas import tpu as pltpu
from jax.sharding import PartitionSpec as P

STEPS = 4
SPAN = 4

DTAU = 0.0625
LAMBDA = 0.5
EPS = 1e-06

VMEM = pl.BlockSpec(memory_space=pltpu.VMEM)
SMEM = pl.BlockSpec(memory_space=pltpu.SMEM)


def from_behind(value, axis, by):
    length = lax.axis_size(axis)
    return lax.ppermute(value, axis, [(i, (i + by) % length) for i in range(length)])


def hopping_kernel(band, table_ref, k_ref):
    sites = table_ref.shape[1]
    rows = [jnp.broadcast_to(table_ref[k : k + 1, :], (band, sites)) for k in range(4)]
    label = lax.broadcasted_iota(jnp.int32, (band, sites), 0)
    for b in range(sites // band):
        hits = jnp.zeros((band, sites), jnp.float32)
        for k in range(4):
            hits = hits + jnp.where(rows[k] == label + b * band, 1.0, 0.0)
        k_ref[b * band : (b + 1) * band, :] = hits.astype(k_ref.dtype)


def hop_kernel(band, k_ref, hop_ref):
    sites = k_ref.shape[0]
    label = lax.broadcasted_iota(jnp.int32, (band, sites), 0)
    column = lax.broadcasted_iota(jnp.int32, (band, sites), 1)
    for b in range(sites // band):
        own = slice(b * band, (b + 1) * band)
        ksq = jnp.dot(k_ref[own, :], k_ref[...], preferred_element_type=jnp.float32)
        eye = jnp.where(column == label + b * band, 1.0, 0.0)
        hop_ref[own, :] = (
            eye + DTAU * k_ref[own, :].astype(jnp.float32) + 0.5 * DTAU * DTAU * ksq
        ).astype(hop_ref.dtype)


def square_kernel(kernel, name, operand, dtype):
    sites = operand.shape[1]
    return pl.pallas_call(
        functools.partial(kernel, 384),
        out_shape=jax.ShapeDtypeStruct((sites, sites), dtype),
        in_specs=[VMEM],
        out_specs=VMEM,
        compiler_params=pltpu.CompilerParams(vmem_limit_bytes=16 << 20),
        name=name,
    )(operand)


def step_kernel(x_ref, hop_ref, spins_ref, out_ref, log_ref):
    factor = jnp.exp(LAMBDA * spins_ref[...].astype(jnp.float32))
    image = passed(x_ref[...], hop_ref, factor, 0)
    image, log = normalized(image)
    log_ref[...] = log.T[0:1, :]
    out_ref[...] = image.astype(out_ref.dtype)


def last_kernel(place_ref, x_ref, hop_ref, spins_ref, out_ref, log_ref, half_ref, sem):
    sign = jnp.where(place_ref[0] < STEPS * SPAN, -1.0, 1.0)
    factor = jnp.exp(LAMBDA * spins_ref[...].astype(jnp.float32))
    current = passed(x_ref[...], hop_ref, factor, 1).astype(jnp.bfloat16)
    rows = current.shape[0] // 2
    copies, logs = [], []
    for h in range(2):
        image = jnp.dot(current[h * rows : (h + 1) * rows], hop_ref[...], preferred_element_type=jnp.float32)
        image, log = normalized(image * factor[SPAN - 1 : SPAN, :])
        half_ref[h] = image * sign
        copies.append(pltpu.make_async_copy(half_ref.at[h], out_ref.at[pl.ds(h * rows, rows)], sem.at[h]))
        copies[h].start()
        logs.append(log)
    log_ref[...] = jnp.concatenate(logs, axis=0).T[0:1, :]
    for copy in copies:
        copy.wait()


def passed(current, hop_ref, factor, left):
    for part in range(SPAN - left):
        image = jnp.dot(current, hop_ref[...], preferred_element_type=jnp.float32)
        image = image * factor[part : part + 1, :]
        current = image.astype(jnp.bfloat16)
    return image


def normalized(image):
    rms = jnp.sqrt(jnp.mean(image * image, axis=1, keepdims=True) + EPS)
    log = jnp.broadcast_to(jnp.log(rms) / (STEPS * SPAN), (rms.shape[0], 128))
    return image * (1.0 / rms), log


def step(number, place, x, hop, group):
    rows, sites = x.shape
    last = number == STEPS - 1
    return pl.pallas_call(
        last_kernel if last else step_kernel,
        out_shape=[
            jax.ShapeDtypeStruct((rows, sites), jnp.float32 if last else jnp.bfloat16),
            jax.ShapeDtypeStruct((1, rows), jnp.float32),
        ],
        in_specs=[SMEM] * last + [VMEM] * 3,
        out_specs=[pl.BlockSpec(memory_space=pl.ANY) if last else VMEM, VMEM],
        scratch_shapes=[pltpu.VMEM((2, rows // 2, sites), jnp.float32), pltpu.SemaphoreType.DMA((2,))] if last else [],
        compiler_params=pltpu.CompilerParams(vmem_limit_bytes=16 << 20),
        name=f"step_{number}",
    )(*([place] if last else []), x, hop, group)


def shards(spins, neighbours, start):
    place = lax.axis_index("tm")[None]
    incoming = from_behind(start.astype(jnp.bfloat16), "tm", STEPS * SPAN)
    row = spins.astype(jnp.bfloat16)
    near = [from_behind(row, "tm", by) for by in (3, 2, 1)]
    hopping = square_kernel(hopping_kernel, "hopping", neighbours.T, jnp.float8_e4m3fn)
    near, hopping = lax.optimization_barrier((near, hopping))
    own = jnp.concatenate(near + [row], axis=0)
    group0 = from_behind(own, "tm", 3 * SPAN)
    group1 = from_behind(own, "tm", 2 * SPAN)
    own, hopping = lax.optimization_barrier((own, hopping))
    hop = square_kernel(hop_kernel, "hop", hopping, jnp.bfloat16)
    group0, group1, hop = lax.optimization_barrier((group0, group1, hop))
    x, log0 = step(0, place, incoming, hop, group0)
    pad = ((0, 0), (0, group0.shape[1] - log0.shape[1]))
    sent = jnp.concatenate([group0.astype(jnp.float32), jnp.pad(log0, pad)], axis=0)
    came = from_behind(sent, "tm", -2 * SPAN)
    group1, x = lax.optimization_barrier((group1, x))
    x, log1 = step(1, place, x, hop, group1)
    middle = from_behind(log1, "tm", -2 * SPAN)
    came, x = lax.optimization_barrier((came, x))
    x, log2 = step(2, place, x, hop, came[:SPAN])
    late = from_behind(jnp.concatenate([log2, came[SPAN:, : log2.shape[1]]], axis=0), "tm", -SPAN)
    panels, log3 = step(3, place, x, hop, own)
    growth = log3[0] + late[0] + late[1] + middle[0]
    return panels, growth


def solution(mesh):
    return jax.shard_map(
        shards,
        mesh=mesh,
        in_specs=(P("tm", None), P(), P(("tm", "panel"), None)),
        out_specs=(P(("tm", "panel"), None), P(("tm", "panel"))),
        check_vma=False,
    )
```

```python
import functools

import jax
import jax.numpy as jnp
from jax import lax
from jax.experimental import pallas as pl
from jax.experimental.pallas import tpu as pltpu
from jax.sharding import PartitionSpec as P

STEPS = 4
SPAN = 4

DTAU = 0.0625
LAMBDA = 0.5
EPS = 1e-06

VMEM = pl.BlockSpec(memory_space=pltpu.VMEM)
SMEM = pl.BlockSpec(memory_space=pltpu.SMEM)


def from_behind(value, axis, by):
    length = lax.axis_size(axis)
    return lax.ppermute(value, axis, [(i, (i + by) % length) for i in range(length)])


def hopping_kernel(band, table_ref, k_ref):
    sites = table_ref.shape[1]
    rows = [jnp.broadcast_to(table_ref[k : k + 1, :], (band, sites)) for k in range(4)]
    label = lax.broadcasted_iota(jnp.int32, (band, sites), 0)
    for b in range(sites // band):
        hits = jnp.zeros((band, sites), jnp.float32)
        for k in range(4):
            hits = hits + jnp.where(rows[k] == label + b * band, 1.0, 0.0)
        k_ref[b * band : (b + 1) * band, :] = hits.astype(k_ref.dtype)


def hop_kernel(band, k_ref, hop_ref):
    sites = k_ref.shape[0]
    label = lax.broadcasted_iota(jnp.int32, (band, sites), 0)
    column = lax.broadcasted_iota(jnp.int32, (band, sites), 1)
    for b in range(sites // band):
        own = slice(b * band, (b + 1) * band)
        ksq = jnp.dot(k_ref[own, :], k_ref[...], preferred_element_type=jnp.float32)
        eye = jnp.where(column == label + b * band, 1.0, 0.0)
        hop_ref[own, :] = (
            eye + DTAU * k_ref[own, :].astype(jnp.float32) + 0.5 * DTAU * DTAU * ksq
        ).astype(hop_ref.dtype)


def square_kernel(kernel, name, operand, dtype):
    sites = operand.shape[1]
    return pl.pallas_call(
        functools.partial(kernel, 384),
        out_shape=jax.ShapeDtypeStruct((sites, sites), dtype),
        in_specs=[VMEM],
        out_specs=VMEM,
        compiler_params=pltpu.CompilerParams(vmem_limit_bytes=16 << 20),
        name=name,
    )(operand)


def lead_kernel(x_ref, hop_ref, out_ref):
    out_ref[...] = jnp.dot(x_ref[...], hop_ref[...], preferred_element_type=jnp.float32)


def step_kernel(first, x_ref, hop_ref, spins_ref, out_ref, log_ref):
    factor = jnp.exp(LAMBDA * spins_ref[...].astype(jnp.float32))
    current = x_ref[...]
    if first:
        current = (current * factor[:1, :]).astype(jnp.bfloat16)
    image = passed(current, hop_ref, factor, first, SPAN)
    image, log = normalized(image)
    log_ref[...] = log.T[0:1, :]
    out_ref[...] = image.astype(out_ref.dtype)


def last_kernel(place_ref, x_ref, hop_ref, spins_ref, out_ref, log_ref, half_ref, sem):
    sign = jnp.where(place_ref[0] < STEPS * SPAN, -1.0, 1.0)
    factor = jnp.exp(LAMBDA * spins_ref[...].astype(jnp.float32))
    current = passed(x_ref[...], hop_ref, factor, 0, SPAN - 1).astype(jnp.bfloat16)
    rows = current.shape[0] // 2
    copies, logs = [], []
    for h in range(2):
        image = jnp.dot(current[h * rows : (h + 1) * rows], hop_ref[...], preferred_element_type=jnp.float32)
        image, log = normalized(image * factor[SPAN - 1 : SPAN, :])
        half_ref[h] = image * sign
        copies.append(pltpu.make_async_copy(half_ref.at[h], out_ref.at[pl.ds(h * rows, rows)], sem.at[h]))
        copies[h].start()
        logs.append(log)
    log_ref[...] = jnp.concatenate(logs, axis=0).T[0:1, :]
    for copy in copies:
        copy.wait()


def passed(current, hop_ref, factor, begin, end):
    for part in range(begin, end):
        image = jnp.dot(current, hop_ref[...], preferred_element_type=jnp.float32)
        image = image * factor[part : part + 1, :]
        current = image.astype(jnp.bfloat16)
    return image


def normalized(image):
    rms = jnp.sqrt(jnp.mean(image * image, axis=1, keepdims=True) + EPS)
    log = jnp.broadcast_to(jnp.log(rms) / (STEPS * SPAN), (rms.shape[0], 128))
    return image * (1.0 / rms), log


def step(number, place, x, hop, group):
    rows, sites = x.shape
    last = number == STEPS - 1
    return pl.pallas_call(
        last_kernel if last else functools.partial(step_kernel, int(number == 0)),
        out_shape=[
            jax.ShapeDtypeStruct((rows, sites), jnp.float32 if last else jnp.bfloat16),
            jax.ShapeDtypeStruct((1, rows), jnp.float32),
        ],
        in_specs=[SMEM] * last + [VMEM] * 3,
        out_specs=[pl.BlockSpec(memory_space=pl.ANY) if last else VMEM, VMEM],
        scratch_shapes=[pltpu.VMEM((2, rows // 2, sites), jnp.float32), pltpu.SemaphoreType.DMA((2,))] if last else [],
        compiler_params=pltpu.CompilerParams(vmem_limit_bytes=16 << 20),
        name=f"step_{number}",
    )(*([place] if last else []), x, hop, group)


def lead(x, hop):
    return pl.pallas_call(
        lead_kernel,
        out_shape=jax.ShapeDtypeStruct(x.shape, jnp.float32),
        in_specs=[VMEM, VMEM],
        out_specs=VMEM,
        compiler_params=pltpu.CompilerParams(vmem_limit_bytes=16 << 20),
        name="lead",
    )(x, hop)


def shards(spins, neighbours, start):
    place = lax.axis_index("tm")[None]
    incoming = from_behind(start.astype(jnp.bfloat16), "tm", STEPS * SPAN)
    row = spins.astype(jnp.bfloat16)
    near = [from_behind(row, "tm", by) for by in (3, 2, 1)]
    hopping = square_kernel(hopping_kernel, "hopping", neighbours.T, jnp.float8_e4m3fn)
    near, hopping = lax.optimization_barrier((near, hopping))
    own = jnp.concatenate(near + [row], axis=0)
    group0 = from_behind(own, "tm", 3 * SPAN)
    group1 = from_behind(own, "tm", 2 * SPAN)
    own, hopping = lax.optimization_barrier((own, hopping))
    hop = square_kernel(hop_kernel, "hop", hopping, jnp.bfloat16)
    ahead = lead(incoming, hop)
    group0, ahead = lax.optimization_barrier((group0, ahead))
    x, log0 = step(0, place, ahead, hop, group0)
    pad = ((0, 0), (0, group0.shape[1] - log0.shape[1]))
    sent = jnp.concatenate([group0.astype(jnp.float32), jnp.pad(log0, pad)], axis=0)
    came = from_behind(sent, "tm", -2 * SPAN)
    group1, x = lax.optimization_barrier((group1, x))
    x, log1 = step(1, place, x, hop, group1)
    middle = from_behind(log1, "tm", -2 * SPAN)
    came, x = lax.optimization_barrier((came, x))
    x, log2 = step(2, place, x, hop, came[:SPAN])
    late = from_behind(jnp.concatenate([log2, came[SPAN:, : log2.shape[1]]], axis=0), "tm", -SPAN)
    panels, log3 = step(3, place, x, hop, own)
    growth = log3[0] + late[0] + late[1] + middle[0]
    return panels, growth


def solution(mesh):
    return jax.shard_map(
        shards,
        mesh=mesh,
        in_specs=(P("tm", None), P(), P(("tm", "panel"), None)),
        out_specs=(P(("tm", "panel"), None), P(("tm", "panel"))),
        check_vma=False,
    )
```
